32 devices in a mesh: dom: 2 (over y), crate: 4 (over z), pair: 2 (over x), sub: 2 (over core).
Axes of the slice: x: 2, y: 2, z: 4, core: 2. Of those that a mesh axis runs over, the one named last changes fastest.
Arguments:
- raw_volts: bfloat16 [512, 71680], P(('dom', 'crate', 'pair', 'sub')), parts along dimension 0, may hold values from -6 to 6
- pair_table: int32 [5, 2], replicated, may hold values from 0 to 1, as said below
- feed_map: int32 [256], replicated, may hold values from 0 to 255, each once
- gains: float32 [1024, 2, 256], P('crate'), may hold values from -0.875 to 0.875
- feed_pos: float32 [2, 256], replicated, may hold values from -8 to 8
- beam_dir: float32 [2, 512], replicated, may hold values from -1 to 1
Outputs:
- beams: float32 [4096, 32, 1024], P(('dom', 'crate', 'pair', 'sub')), parts along dimension 0
The draws below stay inside these ranges and needn't reach their ends.
There are 2 independent parts, one for each index of `dom`. The reference program is written for one: setup_inputs(seed, part) draws one part's arguments, and reference() takes and returns one part's arrays. A program takes and returns all parts, laid end to end along the dimension named above; an argument that names none is the same for every part. Nothing has to cross between parts.
Inputs may be any that keep to these rules, and one draw needn't show every extreme that they name: pair_table[0, p] = p XOR m for every p, with one m of 1 to 1 for the whole row; every other entry is 0 or 1, and pair_table[1 + c, p] + pair_table[1 + c, pair_table[0, p]] = 1 for every board c and position p. feed_map names every feed once.
All inputs are finite; a program needn't handle non-finite values.
Results may differ from the reference program's by a relative error of at most 0.0058.
Values may be sent and summed in bfloat16 or wider, within the bound.
No kernel may reach another device: no remote copies, remote signals or barrier semaphores. Data moves between devices by JAX's collectives and lax.ppermute only.
A program may use at most 64 MiB of HBM per device.

```python
import math
import jax
import jax.numpy as jnp
from jax import lax

INPUTS = 16
NFFT = 2048
TAPS = 4
FRAMES = 32
BEAMS = 512
NCHAN = 1024
FEEDS = 256
SAMPLES = 71680
PAIR_FEEDS = 128
N_CRATE = 4
N_PAIR = 2
N_SUB = 2


def draw_pair_table(key, part):
    offset = jax.random.randint(jax.random.fold_in(key, 1), (), 1, N_PAIR, dtype=jnp.int32)
    position = jnp.arange(N_PAIR, dtype=jnp.int32)
    partner = jnp.bitwise_xor(position, offset).astype(jnp.int32)
    flips = jax.random.randint(jax.random.fold_in(key, 2), (N_CRATE, N_PAIR), 0, 2, dtype=jnp.int32)
    lower = jnp.minimum(position, partner)
    picked = jnp.take(flips, lower, axis=1)
    upper = jnp.where(position[None, :] < partner[None, :], picked, 1 - picked).astype(jnp.int32)
    return jnp.concatenate([partner[None, :], upper], axis=0).astype(jnp.int32)


def steps_of(own_key, extent, cuts, smallest, high):
    gain = 1.0
    for dim, blocks in cuts:
        draws = jax.random.uniform(jax.random.fold_in(jax.random.fold_in(own_key, 6), dim), (blocks,), jnp.float32, smallest / len(cuts), high / len(cuts))
        gain = gain * jnp.repeat(jnp.exp(draws), extent[dim] // blocks).reshape((-1,) + (1,) * (len(extent) - 1 - dim))
    return gain


def gaussian(rng, dims, scale, bound, shards=(), kind=jnp.bfloat16):
    gain = steps_of(rng, dims, shards, -0.22, 0.18) if shards else 1.0
    result = jax.random.normal(rng, dims, jnp.float32) * scale * gain
    return jnp.minimum(jnp.maximum(result, -bound), bound).astype(kind)


def setup_inputs(seed: int = 0, part: int = 0) -> dict:
    key_of = jax.random.split(jax.random.key(seed), 7)
    own_keys = jax.random.split(jax.random.fold_in(key_of[6], part), 7)
    return {
        "raw_volts": gaussian(own_keys[0], (FEEDS, SAMPLES), 1.0, 6.0, ((0, 16),)),
        "pair_table": draw_pair_table(jax.random.fold_in(key_of[6], 71), part),
        "feed_map": jax.random.permutation(key_of[2], FEEDS).astype(jnp.int32),
        "gains": gaussian(key_of[3], (NCHAN, 2, FEEDS), (0.7 * PAIR_FEEDS ** -0.5), 0.875, ((0, 4),), jnp.float32),
        "feed_pos": jnp.clip(jax.random.uniform(key_of[4], (2, FEEDS), jnp.float32, -8.0, 8.0), -8.0, 8.0),
        "beam_dir": jnp.clip(jax.random.uniform(key_of[5], (2, BEAMS), jnp.float32, -1.0, 1.0), -1.0, 1.0),
    }


TWO_PI = 6.283185307179586

def pfb_window():
    span = TAPS * NFFT
    position = jnp.arange(span, dtype=jnp.float32) + 0.5
    shape = jnp.sinc((position - span / 2) / NFFT) * (0.5 - 0.5 * jnp.cos(TWO_PI * position / span))
    return shape.reshape(TAPS, NFFT)

def dft_table():
    sample = jnp.arange(NFFT, dtype=jnp.int32)
    channel = jnp.arange(NCHAN, dtype=jnp.int32)
    phase_index = sample[:, None] * channel[None, :] % NFFT
    angle = phase_index.astype(jnp.float32) * (TWO_PI / NFFT)
    scale = 2.0 / math.sqrt(NFFT)
    value = jnp.concatenate([jnp.cos(angle), -jnp.sin(angle)], axis=1) * scale
    return value.astype(jnp.bfloat16)

def reference(raw_volts, pair_table, feed_map, gains, feed_pos, beam_dir):
    blocks = raw_volts.reshape(FEEDS, FRAMES + TAPS - 1, NFFT)
    window = pfb_window()
    total = window[0][None, None, :] * blocks[:, 0:FRAMES, :].astype(jnp.float32)
    for tap_index in range(1, TAPS):
        total = total + window[tap_index][None, None, :] * blocks[:, tap_index:tap_index + FRAMES, :].astype(jnp.float32)
    windowed = total.astype(jnp.bfloat16).reshape(FEEDS * FRAMES, NFFT)
    spectra = jnp.dot(windowed, dft_table(), preferred_element_type=jnp.float32).astype(jnp.bfloat16)
    spectra = spectra.reshape(FEEDS, FRAMES, 2, NCHAN)
    per_crate = NCHAN // N_CRATE
    half_rows = per_crate // 2
    boards = jnp.arange(N_CRATE, dtype=jnp.int32)
    slots = jnp.arange(INPUTS, dtype=jnp.int32)

    def one_group(group):
        board = group // (N_PAIR * N_SUB)
        crate_pair = group // N_SUB % N_PAIR
        side = group % N_SUB
        partner = pair_table[0, crate_pair]
        upper = pair_table[1 + board, crate_pair].astype(jnp.int32)
        sources = jnp.stack([crate_pair, partner]).astype(jnp.int32)
        rows = (((boards[None, :, None] * N_PAIR + sources[:, None, None]) * N_SUB + side) * INPUTS + slots[None, None, :]).reshape(-1)
        first = (board * per_crate + upper * half_rows).astype(jnp.int32)
        volts = lax.dynamic_slice_in_dim(spectra[rows], first, half_rows, 3)
        feeds = feed_map[rows]
        gain_rows = jnp.take(lax.dynamic_slice_in_dim(gains, first, half_rows, 0), feeds, axis=2)
        place_x = feed_pos[0][feeds]
        place_y = feed_pos[1][feeds]
        dotted = place_x[:, None] * beam_dir[0][None, :] + place_y[:, None] * beam_dir[1][None, :]
        channel = (first + jnp.arange(half_rows, dtype=jnp.int32)).astype(jnp.float32)
        turns = (2 * NCHAN - channel) * (TWO_PI / (2 * NCHAN))
        angle = turns[:, None, None] * dotted[None]
        cosine = jnp.cos(angle)
        sine = jnp.sin(angle)
        real_gain = gain_rows[:, 0][:, :, None]
        imag_gain = gain_rows[:, 1][:, :, None]
        w_real = (real_gain * cosine + imag_gain * sine).astype(jnp.bfloat16).astype(jnp.float32)
        w_imag = (imag_gain * cosine - real_gain * sine).astype(jnp.bfloat16).astype(jnp.float32)
        x_real = volts[:, :, 0, :].astype(jnp.float32)
        x_imag = volts[:, :, 1, :].astype(jnp.float32)
        high = lax.Precision.HIGHEST
        out_real = jnp.einsum('kfq,qkb->qfb', x_real, w_real, precision=high) - jnp.einsum('kfq,qkb->qfb', x_imag, w_imag, precision=high)
        out_imag = jnp.einsum('kfq,qkb->qfb', x_imag, w_real, precision=high) + jnp.einsum('kfq,qkb->qfb', x_real, w_imag, precision=high)
        return jnp.concatenate([out_real, out_imag], axis=-1)
    beams = lax.map(one_group, jnp.arange(N_CRATE * N_PAIR * N_SUB, dtype=jnp.int32))
    return beams.reshape(N_CRATE * N_PAIR * N_SUB * half_rows, FRAMES, 2 * BEAMS)
```

```python
import functools
import math

import numpy as np
import jax
import jax.numpy as jnp
from jax import lax
from jax.experimental import pallas as pl
from jax.experimental.pallas import tpu as pltpu
from jax.sharding import PartitionSpec as P

NFFT = 2048
TAPS = 4
BEAMS = 512
NCHAN = 1024
LANES = 128
TWO_PI = 6.283185307179586
CHUNK = 32
GROUP = 16


def pfb_window():
    span = TAPS * NFFT
    u = np.arange(span, dtype=np.float64) + 0.5
    shape = np.sinc((u - span / 2) / NFFT) * (0.5 - 0.5 * np.cos(2 * np.pi * u / span))
    return shape.reshape(TAPS, NFFT).astype(np.float32)


def base_tables(chunk):
    half = NFFT // 2
    n = np.arange(half)[:, None]
    ch = np.arange(chunk)[None, :]
    a = 2 * np.pi * ((n * ch) % NFFT) / NFFT
    scale = 2.0 / math.sqrt(NFFT)
    re, im = np.cos(a) * scale, -np.sin(a) * scale
    copies = LANES // (2 * chunk)
    straight = np.tile(np.concatenate([re, im], 1), (1, copies))
    crossed = np.tile(np.concatenate([-im, re], 1), (1, copies))
    return straight.astype(np.float32), crossed.astype(np.float32)


def shift_tables(chunk):
    period = NFFT // chunk
    n = np.arange(period)[:, None]
    u = np.arange(LANES)[None, :]
    a = 2 * np.pi * ((n * u) % period) / period
    return np.cos(a).astype(np.float32), (-np.sin(a)).astype(np.float32)


def window_frames(raw_ref, win_ref, win_out, frames, inputs):
    fold = LANES // (2 * CHUNK)
    per = frames // fold

    def column(i, carry):
        cols = pl.ds(pl.multiple_of(i * LANES, LANES), LANES)
        taps = [jnp.broadcast_to(win_ref[t : t + 1, cols], (inputs, LANES)) for t in range(TAPS)]

        def block(b):
            at = pl.ds(pl.multiple_of(b * NFFT + i * LANES, LANES), LANES)
            return raw_ref[:, at].astype(jnp.float32)

        held = [block(b) for b in range(TAPS - 1)]
        for f in range(frames):
            held.append(block(f + TAPS - 1))
            total = taps[0] * held[0]
            for t in range(1, TAPS):
                total = total + taps[t] * held[t]
            held = held[1:]
            row = ((f % fold) * per + f // fold) * inputs
            win_out[row : row + inputs, cols] = total.astype(jnp.bfloat16)
        return carry

    lax.fori_loop(0, NFFT // LANES, column, 0)


def spectra_tiles(first, unit_ref, straight_ref, crossed_ref, sre_ref, sim_ref, windowed, table, outs, fold):
    period = sre_ref.shape[0]
    half = NFFT // 2
    lane = lax.broadcasted_iota(jnp.int32, (LANES, LANES), 1)
    row = lax.broadcasted_iota(jnp.int32, (LANES, LANES), 0)
    wide = LANES // fold
    rotations = []
    for tile in range(2):
        unit = unit_ref[first + tile * fold]
        for d in range(1, fold):
            unit = jnp.where(lane >= d * wide, unit_ref[first + tile * fold + d], unit)
        pick = jnp.where(row == unit, 1.0, 0.0).astype(jnp.float32)
        dot = functools.partial(jnp.dot, precision=lax.Precision.HIGHEST, preferred_element_type=jnp.float32)
        rotations.append((dot(sre_ref[...], pick), dot(sim_ref[...], pick)))
    odd = lax.broadcasted_iota(jnp.int32, (period, LANES), 1) % 2 == 1

    def build(i, carry):
        rows = pl.ds(pl.multiple_of(i * period, period), period)
        upper = pl.ds(pl.multiple_of(half + i * period, period), period)
        straight, crossed = straight_ref[rows, :], crossed_ref[rows, :]
        for tile in range(2):
            re, im = rotations[tile]
            value = re * straight + im * crossed
            lanes = slice(tile * LANES, (tile + 1) * LANES)
            table[rows, lanes] = value.astype(jnp.bfloat16)
            table[upper, lanes] = jnp.where(odd, -value, value).astype(jnp.bfloat16)
        return carry

    lax.fori_loop(0, half // period, build, 0)
    product = jnp.dot(windowed[...], table[...], preferred_element_type=jnp.float32)
    rows = windowed.shape[0] // fold
    at = lax.broadcasted_iota(jnp.int32, (rows, LANES), 1) // wide
    for tile in range(2):
        parts = [product[g * rows : (g + 1) * rows, tile * LANES : (tile + 1) * LANES] for g in range(fold)]
        for d in range(fold):
            value = parts[d]
            for g in range(fold):
                if g != d:
                    moved = pltpu.roll(parts[g], (g - d) % fold * wide, 1)
                    value = jnp.where(at == g, moved, value)
            outs[tile * fold + d][...] = value.astype(jnp.bfloat16)


def first_kernel(frames, slots, unit_ref, raw_ref, win_ref, straight_ref, crossed_ref, sre_ref, sim_ref, *rest):
    outs, windowed, table = rest[:slots], rest[slots], rest[slots + 1]
    fold = LANES // (2 * CHUNK)
    window_frames(raw_ref, win_ref, windowed, frames, raw_ref.shape[0])
    for first in range(0, slots, 2 * fold):
        spectra_tiles(first, unit_ref, straight_ref, crossed_ref, sre_ref, sim_ref, windowed, table,
                      outs[first : first + 2 * fold], fold)


def later_kernel(slots, chunks, unit_ref, windowed, straight_ref, crossed_ref, sre_ref, sim_ref, *rest):
    outs, table = rest[: slots * chunks], rest[slots * chunks]
    fold = LANES // (2 * CHUNK)
    for first in range(0, slots * chunks, 2 * fold):
        spectra_tiles(first, unit_ref, straight_ref, crossed_ref, sre_ref, sim_ref, windowed, table,
                      outs[first : first + 2 * fold], fold)


def spectra_calls(raw_volts, units, frames):
    chunks, slots = len(units), len(units[0])
    inputs = raw_volts.shape[0]
    rows = inputs * frames
    fold = LANES // (2 * CHUNK)
    straight, crossed = base_tables(CHUNK)
    sre, sim = shift_tables(CHUNK)
    consts = (jnp.asarray(straight), jnp.asarray(crossed), jnp.asarray(sre), jnp.asarray(sim))
    vmem = pl.BlockSpec(memory_space=pltpu.VMEM)
    smem = pl.BlockSpec(memory_space=pltpu.SMEM)
    piece = jax.ShapeDtypeStruct((rows // fold, LANES), jnp.bfloat16)
    flops = 2 * rows * NFFT * 2 * CHUNK * slots
    first = pl.pallas_call(
        functools.partial(first_kernel, frames, slots),
        out_shape=[piece] * slots + [jax.ShapeDtypeStruct((rows, NFFT), jnp.bfloat16)],
        in_specs=[smem] + [vmem] * 6,
        out_specs=[vmem] * (slots + 1),
        scratch_shapes=[pltpu.VMEM((NFFT, 2 * LANES), jnp.bfloat16)],
        cost_estimate=pl.CostEstimate(flops=flops, bytes_accessed=8 << 20, transcendentals=0),
        name="spectra_first",
    )(jnp.stack(units[0]), raw_volts, jnp.asarray(pfb_window()), *consts)
    pieces, windowed = [list(first[:slots])], first[slots]
    if chunks > 1:
        more = chunks - 1
        later = pl.pallas_call(
            functools.partial(later_kernel, slots, more),
            out_shape=[piece] * (slots * more),
            in_specs=[smem] + [vmem] * 5,
            out_specs=[vmem] * (slots * more),
            scratch_shapes=[pltpu.VMEM((NFFT, 2 * LANES), jnp.bfloat16)],
            cost_estimate=pl.CostEstimate(flops=flops * more, bytes_accessed=8 << 20, transcendentals=0),
            name="spectra_later",
        )(jnp.stack(sum(units[1:], [])), windowed, *consts)
        for q in range(more):
            pieces.append(list(later[q * slots : (q + 1) * slots]))
    return pieces, windowed


def phasor_kernel(first_ref, dot_ref, near_ref, centre_ref):
    reach = GROUP // 2
    step = TWO_PI / (2 * NCHAN)
    turns = (2 * NCHAN - (first_ref[0] + reach)).astype(jnp.float32) * step

    def rows(i, carry):
        at = pl.ds(pl.multiple_of(i * 8, 8), 8)
        dotted = dot_ref[at, :]
        theta = dotted * step
        c1, s1 = jnp.cos(theta), jnp.sin(theta)
        c, s = c1, s1
        for j in range(reach):
            near_ref[j, 0, at, :] = c
            near_ref[j, 1, at, :] = s
            if j + 1 < reach:
                c, s = c * c1 - s * s1, s * c1 + c * s1
        full_c, full_s = c * c - s * s, 2.0 * s * c
        phase = turns * dotted
        c, s = jnp.cos(phase), jnp.sin(phase)
        for g in range(centre_ref.shape[0]):
            centre_ref[g, 0, at, :] = c
            centre_ref[g, 1, at, :] = s
            c, s = c * full_c + s * full_s, s * full_c - c * full_s
        return carry

    lax.fori_loop(0, dot_ref.shape[0] // 8, rows, 0)


def phasor_call(first_channel, dotted, groups):
    across = dotted.shape[0]
    vmem = pl.BlockSpec(memory_space=pltpu.VMEM)
    return pl.pallas_call(
        phasor_kernel,
        out_shape=[
            jax.ShapeDtypeStruct((GROUP // 2, 2, across, BEAMS), jnp.float32),
            jax.ShapeDtypeStruct((groups, 2, across, BEAMS), jnp.float32),
        ],
        in_specs=[pl.BlockSpec(memory_space=pltpu.SMEM), vmem],
        out_specs=[vmem, vmem],
        cost_estimate=pl.CostEstimate(flops=1 << 28, bytes_accessed=8 << 20, transcendentals=1 << 20),
        name="phasors",
    )(first_channel.reshape(1), dotted)


def beam_kernel(slots, inputs, frames, *refs):
    pieces = refs[:slots]
    gain_ref, near_ref, centre_ref = refs[slots : slots + 3]
    out_ref, fixed, weights = refs[-3:]
    across = slots * inputs
    fold = LANES // (2 * CHUNK)
    reach = GROUP // 2

    @pl.when(pl.program_id(0) == 0)
    def _():
        per = LANES // inputs
        for block in range(across // LANES):
            lanes = slice(block * LANES, (block + 1) * LANES)
            gain_re, gain_im = gain_ref[0, :, lanes], gain_ref[1, :, lanes]

            def turn(i, carry):
                at = pl.ds(pl.multiple_of(i * inputs, inputs), inputs)
                stacked = jnp.concatenate(
                    [pieces[block * per + s][at, :].astype(jnp.float32) for s in range(per)], axis=0
                )
                turned = stacked.T
                for g in range(fold):
                    re = turned[2 * g * CHUNK : (2 * g + 1) * CHUNK]
                    im = turned[(2 * g + 1) * CHUNK : (2 * g + 2) * CHUNK]
                    row = pl.multiple_of((i * fold + g) * CHUNK, CHUNK)
                    fixed[block, pl.ds(row, CHUNK), :] = re * gain_re - im * gain_im
                    fixed[block, pl.ds(frames * CHUNK + row, CHUNK), :] = re * gain_im + im * gain_re
                return carry

            lax.fori_loop(0, frames // fold, turn, 0)

    def build(i, carry):
        at = pl.ds(pl.multiple_of(i * 16, 16), 16)
        below = pl.ds(pl.multiple_of(across + i * 16, 16), 16)
        for col in range(BEAMS // LANES):
            cols = slice(col * LANES, (col + 1) * LANES)
            c, s = centre_ref[0, 0, at, cols], centre_ref[0, 1, at, cols]
            weights[reach, at, cols] = c.astype(jnp.bfloat16)
            weights[reach, below, cols] = s.astype(jnp.bfloat16)
            for j in range(1, reach + 1):
                cj, sj = near_ref[j - 1, 0, at, cols], near_ref[j - 1, 1, at, cols]
                cc, ss, sc, cs = c * cj, s * sj, s * cj, c * sj
                weights[reach - j, at, cols] = (cc - ss).astype(jnp.bfloat16)
                weights[reach - j, below, cols] = (sc + cs).astype(jnp.bfloat16)
                if j < reach:
                    weights[reach + j, at, cols] = (cc + ss).astype(jnp.bfloat16)
                    weights[reach + j, below, cols] = (sc - cs).astype(jnp.bfloat16)
        return carry

    lax.fori_loop(0, across // 16, build, 0)

    def channel(i, carry):
        ch = pl.program_id(0) * GROUP + i
        re = [fixed[b, pl.ds(ch, frames, stride=CHUNK), :] for b in range(across // LANES)]
        im = [fixed[b, pl.ds(frames * CHUNK + ch, frames, stride=CHUNK), :] for b in range(across // LANES)]
        left = jnp.concatenate(
            [jnp.concatenate(re + im, axis=1), jnp.concatenate(im + [-x for x in re], axis=1)], axis=0
        ).astype(jnp.bfloat16)
        formed = jnp.dot(left, weights[i], preferred_element_type=jnp.float32)
        out_ref[i, :, :BEAMS] = formed[:frames]
        out_ref[i, :, BEAMS:] = formed[frames:]
        return carry

    lax.fori_loop(0, GROUP, channel, 0, unroll=4)


def beam_call(chunk, pieces, gain, near, centre, previous, half_rows, inputs, frames):
    slots = len(pieces)
    across = slots * inputs
    steps = CHUNK // GROUP
    whole = pl.BlockSpec(memory_space=pltpu.VMEM)
    in_specs = [whole] * slots + [
        pl.BlockSpec((2, CHUNK, across), lambda i: (0, chunk, 0)),
        whole,
        pl.BlockSpec((1, 2, across, BEAMS), lambda i: (chunk * steps + i, 0, 0, 0)),
    ]
    args = [*pieces, gain, near, centre]
    aliases = {}
    if previous is not None:
        in_specs.append(pl.BlockSpec(memory_space=pl.ANY))
        aliases = {len(args): 0}
        args.append(previous)
    return pl.pallas_call(
        functools.partial(beam_kernel, slots, inputs, frames),
        grid=(steps,),
        out_shape=jax.ShapeDtypeStruct((half_rows, frames, 2 * BEAMS), jnp.float32),
        in_specs=in_specs,
        out_specs=pl.BlockSpec((GROUP, frames, 2 * BEAMS), lambda i: (chunk * steps + i, 0, 0)),
        scratch_shapes=[
            pltpu.VMEM((across // LANES, 2 * frames * CHUNK, LANES), jnp.float32),
            pltpu.VMEM((GROUP, 2 * across, BEAMS), jnp.bfloat16),
        ],
        input_output_aliases=aliases,
        cost_estimate=pl.CostEstimate(
            flops=CHUNK * 2 * 2 * frames * 2 * across * BEAMS, bytes_accessed=12 << 20, transcendentals=0
        ),
        name="beams",
    )(*args)


def exchange(pieces, crate_count, pair_count, offset):
    arrived = []
    for chunk in pieces:
        got = []
        for slot, piece in enumerate(chunk):
            a, b = slot // 2, slot % 2
            if slot == 0:
                got.append(piece)
                continue
            move = [
                (c * pair_count + p, (c ^ a) * pair_count + (p ^ (b * offset)))
                for c in range(crate_count)
                for p in range(pair_count)
            ]
            got.append(lax.ppermute(piece, ("crate", "pair"), move))
        arrived.append(got)
    return arrived


def shards(raw_volts, pair_table, feed_map, gains, feed_pos, beam_dir):
    inputs = raw_volts.shape[0]
    frames = raw_volts.shape[1] // NFFT - (TAPS - 1)
    crate_count = lax.axis_size("crate")
    pair_count = lax.axis_size("pair")
    sub_count = lax.axis_size("sub")
    per_crate = NCHAN // crate_count
    half_rows = per_crate // 2
    chunks = half_rows // CHUNK
    board = lax.axis_index("crate")
    crate_pair = lax.axis_index("pair")
    side = lax.axis_index("sub")
    partner = pair_table[0, crate_pair]
    ends = [crate_pair, partner]
    slots = [(a, b) for a in range(crate_count) for b in range(2)]
    starts = []
    for a, b in slots:
        other = board ^ a
        starts.append(other * per_crate + pair_table[1 + other, ends[b]] * half_rows)
    units = [[start // CHUNK + q for start in starts] for q in range(chunks)]
    pieces, windowed = spectra_calls(raw_volts, units, frames)
    if pair_count == 2:
        arrived = exchange(pieces, crate_count, pair_count, 1)
    else:
        arrived = lax.switch(
            pair_table[0, 0] - 1,
            [functools.partial(exchange, crate_count=crate_count, pair_count=pair_count, offset=m)
             for m in range(1, pair_count)],
            pieces,
        )
    feed_map, gains, feed_pos, beam_dir, _ = lax.optimization_barrier(
        (feed_map, gains, feed_pos, beam_dir, windowed)
    )
    rows = jnp.stack([((board ^ a) * pair_count + ends[b]) * sub_count + side for a, b in slots])
    rows = (rows[:, None] * inputs + jnp.arange(inputs, dtype=jnp.int32)[None, :]).reshape(-1)
    feeds = jnp.take(feed_map, rows, axis=0)
    upper = pair_table[1 + board, crate_pair]
    gains_half = lax.dynamic_slice_in_dim(gains, upper * half_rows, half_rows, 0)
    gain = jnp.take(gains_half, feeds, axis=2).transpose(1, 0, 2)
    place = jnp.take(feed_pos, feeds, axis=1)
    dotted = place[0][:, None] * beam_dir[0][None, :] + place[1][:, None] * beam_dir[1][None, :]
    first_channel = board * per_crate + upper * half_rows
    near, centre = phasor_call(first_channel, dotted, half_rows // GROUP)
    out = None
    for q in range(chunks):
        out = beam_call(q, arrived[q], gain, near, centre, out, half_rows, inputs, frames)
    return out


def solution(mesh):
    placed = (P(("dom", "crate", "pair", "sub"), None), P(), P(), P("crate", None, None), P(), P())
    return jax.shard_map(
        shards,
        mesh=mesh,
        in_specs=placed,
        out_specs=P(("dom", "crate", "pair", "sub"), None, None),
        check_vma=False,
    )
```
